32 devices in a mesh: seq: 8 (over z, x), head: 4 (over y, core).
Axes of the slice: x: 2, y: 2, z: 4, core: 2. Of those that a mesh axis runs over, the one named last changes fastest.
Arguments:
- queries: float32 [2048, 8192], P('seq', 'head'), may hold values from -8 to 8
- key_heads: float32 [2048, 1024], P('seq', 'head'), may hold values from -6 to 6
- value_heads: float32 [2048, 1024], P('seq', 'head'), may hold values from -6 to 6
- query_map: float32 [64, 128, 128], P('head'), may hold values from -0.5 to 0.5
- key_map: float32 [8, 128, 128], P('head'), may hold values from -0.5 to 0.5
Outputs:
- query_map_step: float32 [64, 128, 128], P('head')
- key_map_step: float32 [8, 128, 128], P('head')
The draws below stay inside these ranges and needn't reach their ends.
All inputs are finite; a program needn't handle non-finite values.
Results may differ from the reference program's by a relative error of at most 0.00019.
Values sent between devices are 32-bit elements; how exact they have to be, the bound alone decides.
No kernel may reach another device: no remote copies, remote signals or barrier semaphores. Data moves between devices by JAX's collectives and lax.ppermute only.
A program may use at most 64 MiB of HBM per device.

```python
import jax
import jax.numpy as jnp
from jax import lax

HEADS = 64
KV = 8
DH = 128
FEAT = 128
TOKENS = 2048


def paired_draw(key):
    seeded = jax.random.fold_in(key, 7321)
    key_one, key_two = jax.random.split(seeded, 2)
    query_vals = jnp.clip(jax.random.normal(key_one, (TOKENS, HEADS, DH), jnp.float32), -6.0, 6.0)
    key_vals = jnp.clip(jax.random.normal(key_two, (TOKENS, KV, DH), jnp.float32), -6.0, 6.0)
    return (query_vals.reshape(TOKENS, HEADS * DH), key_vals.reshape(TOKENS, KV * DH))


def draw_queries(key, part):
    return paired_draw(key)[0]


def draw_key_heads(key, part):
    return paired_draw(key)[1]


def steps_of(key, extent, pieces, least, largest):
    loudness = 1.0
    for axis_at, parts in pieces:
        heights = jax.random.uniform(jax.random.fold_in(jax.random.fold_in(key, 6), axis_at), (parts,), jnp.float32, least / len(pieces), largest / len(pieces))
        loudness = loudness * jnp.repeat(jnp.exp(heights), extent[axis_at] // parts).reshape((-1,) + (1,) * (len(extent) - 1 - axis_at))
    return loudness


def scatter_about(stream_key, extent, scale, bound, cuts=(), kind=jnp.bfloat16):
    result = scale * jax.random.normal(stream_key, extent, jnp.float32)
    if cuts:
        result = result * steps_of(stream_key, extent, cuts, -0.22, 0.18)
    return jnp.clip(result, -bound, bound).astype(kind)


def setup_inputs(seed: int = 0) -> dict:
    streams_of = jax.random.split(jax.random.key(seed), 6)
    queries = draw_queries(jax.random.fold_in(streams_of[5], 71), 0)
    key_heads = draw_key_heads(jax.random.fold_in(streams_of[5], 71), 0)
    value_heads = scatter_about(streams_of[2], (TOKENS, KV * DH), 1.0, 6.0, ((0, 8), (1, 4)), jnp.float32)
    query_map = scatter_about(streams_of[3], (HEADS, DH, FEAT), DH ** -0.5, 0.5, ((0, 4),), jnp.float32)
    key_map = scatter_about(streams_of[4], (KV, DH, FEAT), DH ** -0.5, 0.5, ((0, 4),), jnp.float32)
    return {"queries": queries, "key_heads": key_heads, "value_heads": value_heads, "query_map": query_map, "key_map": key_map}


HIGHEST = lax.Precision.HIGHEST
NEGATIVE = -1e+30
EPSILON = 1e-06

def head_grads(operands):
    query_head, key_head, value_head, query_weight, key_weight = operands
    positions = jnp.arange(TOKENS)
    causal = positions[:, None] >= positions[None, :]
    scores = jnp.dot(query_head, key_head.T, precision=HIGHEST) * DH ** (-0.5)
    masked = jnp.where(causal, scores, NEGATIVE)
    row_top = lax.optimization_barrier(jnp.max(masked, axis=1, keepdims=True))
    weights = jnp.where(causal, jnp.exp(masked - row_top), 0.0)
    teacher = jnp.dot(weights, value_head, precision=HIGHEST) / lax.optimization_barrier(jnp.sum(weights, axis=1, keepdims=True))

    def loss_of(query_map_head, key_map_head):
        query_feat = jax.nn.softplus(jnp.dot(query_head, query_map_head, precision=HIGHEST))
        key_feat = jax.nn.softplus(jnp.dot(key_head, key_map_head, precision=HIGHEST))
        kernel = jnp.where(causal, jnp.dot(query_feat, key_feat.T, precision=HIGHEST), 0.0)
        student = jnp.dot(kernel, value_head, precision=HIGHEST) / lax.optimization_barrier(jnp.sum(kernel, axis=1, keepdims=True))
        return 0.5 * jnp.sum((student - teacher) ** 2)
    return jax.grad(loss_of, argnums=(0, 1))(query_weight, key_weight)

def reference(queries, key_heads, value_heads, query_map, key_map):
    group_size = HEADS // KV
    query_split = queries.reshape(TOKENS, HEADS, DH).transpose(1, 0, 2)
    key_split = key_heads.reshape(TOKENS, KV, DH).transpose(1, 0, 2)
    value_split = value_heads.reshape(TOKENS, KV, DH).transpose(1, 0, 2)
    key_repeat = jnp.repeat(key_split, group_size, axis=0)
    value_repeat = jnp.repeat(value_split, group_size, axis=0)
    map_repeat = jnp.repeat(key_map, group_size, axis=0)
    grad_query, grad_key_heads = lax.map(head_grads, (query_split, key_repeat, value_repeat, query_map, map_repeat))
    grad_key = lax.optimization_barrier(jnp.sum(grad_key_heads.reshape(KV, group_size, DH, FEAT), axis=1))
    mean_square = (jnp.sum(grad_query * grad_query) + jnp.sum(grad_key * grad_key)) / ((HEADS + KV) * DH * FEAT)
    factor = 1.0 / jnp.sqrt(mean_square + EPSILON)
    return (grad_query * factor, grad_key * factor)
```

```python
import functools
import math

import jax
import jax.numpy as jnp
from jax import lax
from jax.experimental import pallas as pl
from jax.experimental.pallas import tpu as pltpu
from jax.sharding import PartitionSpec as P

EPSILON = 1e-06
F32 = jnp.float32
BF16 = jnp.bfloat16
LIMIT = 20 * 2**20
NN = (((1,), (0,)), ((), ()))
TN = (((0,), (0,)), ((), ()))


def split(x):
    hi = x.astype(BF16)
    lo = (x - hi.astype(F32)).astype(BF16)
    return hi, lo


def mm(a, b, dims=NN):
    return lax.dot_general(a, b, dims, preferred_element_type=F32)


def wide(x):
    return jnp.concatenate(split(x), axis=1)


def tall(hi):
    return jnp.concatenate([hi, hi], axis=0)


def fold(x):
    half = x.shape[1] // 2
    return x[:, :half] + x[:, half:]


def square(x):
    return tall(wide(x))


def softplus(x):
    return jnp.maximum(x, 0.0) + jnp.log1p(jnp.exp(-jnp.abs(x)))


def sigmoid(x):
    e = jnp.exp(-jnp.abs(x))
    r = 1.0 / (1.0 + e)
    return jnp.where(x >= 0.0, r, e * r)


def row_sum(x):
    return jnp.sum(x, axis=1, keepdims=True)


def attend_kernel(first, count, groups, pair, scale, flags, *refs):
    q_ref = refs[0]
    blocks = refs[1 : 1 + count]
    if first:
        qt_ref, stat_out, acc_out = refs[1 + count : 4 + count]
        keys, vals = refs[4 + count :]
    else:
        wk_ref, stat_in, acc_in, st_in, nm_in = refs[1 + count : 6 + count]
        stat_out, acc_out, st_out, nm_out, sig_out = refs[6 + count : 11 + count]
        keys, vals = refs[11 + count :]
    rows = blocks[0].shape[0]
    dh = blocks[0].shape[1] // (2 * groups)
    heads = acc_out.shape[0]
    steps = heads // groups // pair
    on = flags[0]
    for b in range(1, count):
        on = on + flags[b]

    def prepare(b):
        for g in range(groups):
            kv = blocks[b][:, 2 * g * dh : 2 * (g + 1) * dh]
            key_wide = wide(kv[:, :dh])
            keys[g, b * rows : (b + 1) * rows, :] = key_wide
            vals[g, :, b * rows : (b + 1) * rows] = jnp.concatenate(split(kv[:, dh:].T), axis=0)
            if not first:
                act = fold(mm(key_wide, square(wk_ref[g])))
                sig_out[b, g] = sigmoid(act)
                feat = softplus(act)
                fh, fl = split(feat)
                val_wide = wide(kv[:, dh:])
                st_out[g] += fold(mm(fh, val_wide, TN)) + mm(fl, val_wide[:, :dh], TN)
                nm_out[g] += jnp.sum(feat.reshape(-1, 8, feat.shape[1]), axis=0)

    def update(begin, number):
        def some_heads(j, _):
            g = lax.div(j, steps)

            def scores(p):
                h = j * pair + p
                if first:
                    q = q_ref[:, pl.ds(pl.multiple_of(h * dh, dh), dh)] * scale
                    q_t = jnp.concatenate(split(q.T), axis=0)
                    qt_ref[h] = q_t
                else:
                    q_t = q_ref[h]
                q_hi, q_lo = tall(q_t[:dh]), q_t[dh:]
                found = []
                for b in range(number):
                    key = keys[g, (begin + b) * rows : (begin + b + 1) * rows, :]
                    s = mm(key, q_hi) + mm(key[:, :dh], q_lo)
                    if first:
                        before = lax.broadcasted_iota(jnp.int32, s.shape, 0) <= lax.broadcasted_iota(jnp.int32, s.shape, 1)
                        s = jnp.where(before, s, -1e30)
                    found.append(s)
                return found

            ahead = scores(0)
            for p in range(pair):
                h = j * pair + p
                now = ahead
                new = functools.reduce(jnp.maximum, [jnp.max(s, axis=0, keepdims=True) for s in now])
                if not first:
                    old = stat_out[h, 0:1, :]
                    new = jnp.maximum(old, new)
                    fade = jnp.exp2(old - new)
                if p + 1 < pair:
                    ahead = scores(p + 1)
                tot, out = 0.0, 0.0
                for b in range(number):
                    w = jnp.exp2(now[b] - new)
                    tot = tot + jnp.sum(w, axis=0, keepdims=True)
                    wh, wl = split(w)
                    val = vals[g, :, (begin + b) * rows : (begin + b + 1) * rows]
                    both = mm(val, wh)
                    out = out + both[:dh] + both[dh:] + mm(val[:dh], wl)
                if not first:
                    tot = tot + fade * stat_out[h, 1:2, :]
                    out = out + fade * acc_out[h]
                stat_out[h, 0:1, :] = new
                stat_out[h, 1:2, :] = tot
                acc_out[h] = out
            return 0

        lax.fori_loop(0, heads // pair, some_heads, 0)

    if first:
        prepare(0)
        update(0, 1)
        return

    @pl.when(on == count)
    def _():
        for b in range(count):
            prepare(b)
        update(0, count)

    if count > 1:
        for b in range(count):

            @pl.when(jnp.logical_and(on < count, flags[b] > 0))
            def _():
                prepare(b)
                update(b, 1)


def attend(q, blocks, flags, key_map, state, heads, pair):
    groups, dh, feat = key_map.shape
    rows = blocks[0].shape[0]
    count = len(blocks)
    first = state is None
    stat_shape = jax.ShapeDtypeStruct((heads, 2, rows), F32)
    acc_shape = jax.ShapeDtypeStruct((heads, dh, rows), F32)
    vmem = pl.BlockSpec(memory_space=pltpu.VMEM)
    smem = pl.BlockSpec(memory_space=pltpu.SMEM)
    alias = {}
    if first:
        args = [q, *blocks]
        out_shape = [jax.ShapeDtypeStruct((heads, 2 * dh, rows), BF16), stat_shape, acc_shape]
    else:
        args = [q, *blocks, key_map, *state]
        out_shape = [
            stat_shape,
            acc_shape,
            jax.ShapeDtypeStruct((groups, feat, dh), F32),
            jax.ShapeDtypeStruct((groups, 8, feat), F32),
            jax.ShapeDtypeStruct((count, groups, rows, feat), F32),
        ]
        alias = {3 + count + i: i for i in range(4)}
    scale = math.log2(math.e) * dh ** (-0.5)
    return pl.pallas_call(
        functools.partial(attend_kernel, first, count, groups, pair, scale),
        out_shape=out_shape,
        in_specs=[smem] + [vmem] * len(args),
        out_specs=[vmem] * len(out_shape),
        scratch_shapes=[
            pltpu.VMEM((groups, count * rows, 2 * dh), BF16),
            pltpu.VMEM((groups, 2 * dh, count * rows), BF16),
        ],
        input_output_aliases=alias,
        compiler_params=pltpu.CompilerParams(vmem_limit_bytes=LIMIT),
        cost_estimate=pl.CostEstimate(
            flops=heads * count * 24 * rows * rows * dh,
            bytes_accessed=4 * rows * dh * heads * 3,
            transcendentals=heads * count * rows * rows,
        ),
        name="attend",
    )(flags, *args)


def causal_mask(rows):
    return lax.broadcasted_iota(jnp.int32, (rows, rows), 0) >= lax.broadcasted_iota(jnp.int32, (rows, rows), 1)


def local_kernel(groups, pair, *refs):
    q_ref, kv_ref, wq_ref, wk_ref, qf_ref, sig_ref, num_ref, part_ref, feat_ref, sig_k_ref, turned, turned_lo, val_w = refs
    heads, dh, feat_dim = wq_ref.shape
    rows = q_ref.shape[0]
    steps = heads // groups // pair
    for g in range(groups):
        kv = kv_ref[:, 2 * g * dh : 2 * (g + 1) * dh]
        act = fold(mm(wide(kv[:, :dh]), square(wk_ref[g])))
        feat = softplus(act)
        sig_k_ref[g] = sigmoid(act)
        hi, lo = split(feat.T)
        turned[g] = tall(hi)
        turned_lo[g] = lo
        feat_ref[g] = wide(feat)
        val_w[g] = wide(kv[:, dh:])
    causal = causal_mask(rows)

    def some_heads(j, _):
        g = lax.div(j, steps)
        each = [j * pair + p for p in range(pair)]
        q = [wide(q_ref[:, pl.ds(pl.multiple_of(h * dh, dh), dh)]) for h in each]
        act = [fold(mm(x, square(wq_ref[h]))) for x, h in zip(q, each)]
        qf = [wide(softplus(x)) for x in act]
        for x, y, h in zip(act, qf, each):
            sig_ref[h] = sigmoid(x)
            qf_ref[h] = y
        kern = [mm(x, turned[g]) + mm(x[:, :feat_dim], turned_lo[g]) for x in qf]
        kern = [jnp.where(causal, x, 0.0) for x in kern]
        for x, h in zip(kern, each):
            part_ref[h] = functools.reduce(
                jnp.add, [x[:, c : c + feat_dim] for c in range(0, rows, feat_dim)]
            )
        halves = [split(x) for x in kern]
        val = val_w[g]
        for (hi, lo), h in zip(halves, each):
            num_ref[h] = fold(mm(hi, val)) + mm(lo, val[:, :dh])
        return 0

    lax.fori_loop(0, heads // pair, some_heads, 0)


def vmem_call(kernel, args, out_shape, scratch, flops, name, first_smem=True):
    vmem = pl.BlockSpec(memory_space=pltpu.VMEM)
    smem = pl.BlockSpec(memory_space=pltpu.SMEM)
    return pl.pallas_call(
        kernel,
        out_shape=out_shape,
        in_specs=([smem] if first_smem else [vmem]) + [vmem] * (len(args) - 1),
        out_specs=[vmem] * len(out_shape),
        scratch_shapes=scratch,
        compiler_params=pltpu.CompilerParams(vmem_limit_bytes=LIMIT),
        cost_estimate=pl.CostEstimate(flops=flops, bytes_accessed=2**22, transcendentals=2**20),
        name=name,
    )(*args)


def local(q, own, query_map, key_map, pair):
    heads, dh, feat = query_map.shape
    groups = key_map.shape[0]
    rows = q.shape[0]
    shape = jax.ShapeDtypeStruct
    return vmem_call(
        functools.partial(local_kernel, groups, pair),
        [q, own, query_map, key_map],
        [
            shape((heads, rows, 2 * feat), BF16),
            shape((heads, rows, feat), F32),
            shape((heads, rows, dh), F32),
            shape((heads, rows, feat), F32),
            shape((groups, rows, 2 * feat), BF16),
            shape((groups, rows, feat), F32),
        ],
        [
            pltpu.VMEM((groups, 2 * feat, rows), BF16),
            pltpu.VMEM((groups, feat, rows), BF16),
            pltpu.VMEM((groups, rows, 2 * dh), BF16),
        ],
        heads * 24 * rows * rows * dh,
        "local",
        first_smem=False,
    )


def learn_kernel(group, groups, counts, pair, outer, inner, flags, *refs):
    count = sum(counts)
    q_ref, kv_ref, st_ref, nm_ref, stat_ref, acc_ref = refs[:6]
    qf_ref, sig_ref, num_ref, part_ref, feat_ref, sig_k_ref = refs[6:12]
    blocks = refs[12 : 12 + count]
    sigs = refs[12 + count : 12 + count + len(counts)]
    outs = refs[12 + count + len(counts) : 12 + count + len(counts) + inner]
    val_t2, val_t_lo, st_sq, st_t_sq, adj, adj_n, result = refs[12 + count + len(counts) + inner :]
    heads, rows, dh = num_ref.shape
    feat_dim = sig_ref.shape[2]
    ratio = heads // groups
    total = outer * inner
    q_rows, k_rows = ratio * dh // total, dh // total
    outer_me, inner_me = flags[count], flags[count + 1]
    columns = slice(2 * group * dh, (2 * group + 1) * dh)
    val_columns = slice((2 * group + 1) * dh, 2 * (group + 1) * dh)

    def place(s):
        i, j = lax.div(s, inner), lax.rem(s, inner)
        return lax.rem(j - inner_me + inner, inner), lax.rem(i - outer_me + outer, outer)

    hi, lo = split(kv_ref[:, val_columns].T)
    val_t2[...] = tall(hi)
    val_t_lo[...] = lo
    st_sq[...] = square(st_ref[group])
    st_t_sq[...] = square(st_ref[group].T)
    adj[...] = jnp.zeros_like(adj)
    adj_n[...] = jnp.zeros_like(adj_n)
    norm_prev = jnp.sum(nm_ref[group], axis=0, keepdims=True)
    causal = causal_mask(rows)

    def some_heads(j, _):
        each = [group * ratio + j * pair + p for p in range(pair)]
        teacher = [(acc_ref[h] / stat_ref[h, 1:2, :]).T for h in each]
        qfw = [qf_ref[h] for h in each]
        qf = [x[:, :feat_dim].astype(F32) + x[:, feat_dim:].astype(F32) for x in qfw]
        num = [num_ref[h] + fold(mm(x, st_sq[...])) for x, h in zip(qfw, each)]
        inv = [1.0 / row_sum(part_ref[h] + x * norm_prev) for x, h in zip(qf, each)]
        student = [x * y for x, y in zip(num, inv)]
        mismatch = [x - y for x, y in zip(student, teacher)]
        gn = [wide(x * y) for x, y in zip(mismatch, inv)]
        gd = [-row_sum(x * y) * z for x, y, z in zip(mismatch, student, inv)]
        coupling = [mm(x, val_t2[...]) + mm(x[:, :dh], val_t_lo[...]) for x in gn]
        coupling = [split(jnp.where(causal, x + y, 0.0)) for x, y in zip(coupling, gd)]
        feat = feat_ref[group]
        gqf = [
            fold(mm(hi, feat)) + mm(lo, feat[:, :feat_dim]) + fold(mm(x, st_t_sq[...])) + y * norm_prev
            for (hi, lo), x, y in zip(coupling, gn, gd)
        ]
        for (hi, lo), x, y in zip(coupling, gn, qfw):
            left_hi = jnp.concatenate([hi, x[:, :dh]], axis=1)
            left_lo = jnp.concatenate([lo, x[:, dh:]], axis=1)
            adj[...] += fold(mm(left_hi, y, TN)) + mm(left_lo, y[:, :feat_dim], TN)
        for x, y in zip(qf, gd):
            adj_n[...] += jnp.sum((x * y).reshape(-1, 8, feat_dim), axis=0)
        back = [wide(x * sig_ref[h]) for x, h in zip(gqf, each)]
        for p, (x, h) in enumerate(zip(back, each)):
            hi, lo = split(q_ref[:, pl.ds(pl.multiple_of(h * dh, dh), dh)])
            grad = fold(mm(hi, x, TN)) + mm(lo, x[:, :feat_dim], TN)
            first = (j * pair + p) * (dh // q_rows)
            for k in range(dh // q_rows):
                e, f = place(first + k)
                result[e, f, :q_rows, :] = grad[k * q_rows : (k + 1) * q_rows]
        return 0

    lax.fori_loop(0, ratio // pair, some_heads, 0)

    def key_side(keys, x):
        xw = wide(x)
        hi, lo = split(keys)
        return fold(mm(hi, xw, TN)) + mm(lo, xw[:, :feat_dim], TN)

    adj_sq = square(adj[rows:])
    adj_norm = jnp.sum(adj_n[...], axis=0, keepdims=True)
    grad_k = key_side(kv_ref[:, columns], adj[:rows] * sig_k_ref[group])
    b = 0
    for stage, number in enumerate(counts):
        for k in range(number):
            grad = fold(mm(wide(blocks[b][:, val_columns]), adj_sq)) + adj_norm
            more = key_side(blocks[b][:, columns], grad * sigs[stage][k, group])
            grad_k = grad_k + jnp.where(flags[b] > 0, more, 0.0)
            b += 1
    for s in range(total):
        e, f = place(s)
        result[e, f, q_rows:, :] = grad_k[s * k_rows : (s + 1) * k_rows]
    for e in range(inner):
        outs[e][...] = result[e]


def learn(group, flags, q, own, state, mine, blocks, sigs, sizes, pair):
    groups, heads, outer, inner, dh, feat = sizes
    rows = own.shape[0]
    total = outer * inner
    share = (heads // groups + 1) * dh // total
    counts = tuple(x.shape[0] for x in sigs)
    stat, acc, st, nm = state
    args = [flags, q, own, st, nm, stat, acc, *mine, *blocks, *sigs]
    return vmem_call(
        functools.partial(learn_kernel, group, groups, counts, pair, outer, inner),
        args,
        [jax.ShapeDtypeStruct((outer, share, feat), F32)] * inner,
        [
            pltpu.VMEM((2 * dh, rows), BF16),
            pltpu.VMEM((dh, rows), BF16),
            pltpu.VMEM((2 * feat, 2 * dh), BF16),
            pltpu.VMEM((2 * dh, 2 * feat), BF16),
            pltpu.VMEM((rows + dh, feat), F32),
            pltpu.VMEM((8, feat), F32),
            pltpu.VMEM((inner, outer, share, feat), F32),
        ],
        heads // groups * 40 * rows * rows * dh,
        f"learn{group}",
    )


def piece_kernel(*refs):
    out = refs[-1]
    rows = refs[0].shape[0]
    value = functools.reduce(jnp.add, [r[...] for r in refs[:-1]])
    out[:rows, :] = value
    squares = jnp.sum((value * value).reshape(-1, 8, value.shape[1]), axis=0)
    out[rows:, :] = squares


def finish_kernel(groups, inner, outer, q_rows, k_rows, count, where, *refs):
    squares = refs[0]
    lines = refs[1 : 1 + groups * inner]
    gq_ref, gk_ref = refs[1 + groups * inner :]
    mean = jnp.sum(jnp.sum(squares[...], axis=0, keepdims=True), axis=1, keepdims=True) / count
    factor = 1.0 / jnp.sqrt(mean + EPSILON)
    total = outer * inner
    for g in range(groups):
        for e in range(inner):
            for f in range(outer):
                i = lax.rem(where[0] - f + outer, outer)
                j = lax.rem(where[1] - e + inner, inner)
                s = i * inner + j
                line = lines[g * inner + e]
                q_at = pl.multiple_of((g * total + s) * q_rows, q_rows)
                k_at = pl.multiple_of((g * total + s) * k_rows, k_rows)
                gq_ref[pl.ds(q_at, q_rows), :] = line[f, :q_rows, :] * factor
                gk_ref[pl.ds(k_at, k_rows), :] = line[f, q_rows : q_rows + k_rows, :] * factor


def butterfly(value, axis):
    size = lax.axis_size(axis)
    hop = 1
    while hop < size:
        value = value + lax.ppermute(value, axis, [(s, s ^ hop) for s in range(size)])
        hop *= 2
    return value


def on_device(queries, key_heads, value_heads, query_map, key_map):
    heads = query_map.shape[0]
    groups, dh, feat = key_map.shape
    rows = queries.shape[0]
    ratio = heads // groups
    pair = 2 if ratio % 2 == 0 else 1
    total = lax.axis_size("seq")
    inner = 1 << ((total.bit_length() - 1) // 2)
    outer = total // inner
    me = lax.axis_index("seq")
    outer_me, inner_me = me // inner, me % inner
    at = lambda i, j: i * inner + j
    both = (key_heads.reshape(rows, groups, dh), value_heads.reshape(rows, groups, dh))
    own = jnp.stack(both, axis=2).reshape(rows, groups * 2 * dh)

    along, across = [], []
    moving = own
    for i in range(outer):
        if i > 0:
            pairs = [(at(p, j), at(p + 1, j)) for p in range(i - 1, outer - 1) for j in range(inner)]
            moving = lax.ppermute(moving, "seq", pairs)
        along.append((moving, outer_me >= i))
        side = []
        for d in range(1, inner):
            pairs = [
                (at(p, (j + d) % inner), at(p, j))
                for p in range(i, outer)
                for j in range(inner)
                if i > 0 or (j + d) % inner < j
            ]
            flag = outer_me >= i if i > 0 else (inner_me + d) % inner < inner_me
            side.append((lax.ppermute(moving, "seq", pairs), flag))
        across.append(side)

    always = jnp.ones((1,), jnp.int32)
    turned, stat, acc = attend(queries, [own], always, key_map, None, heads, 4)
    state = [stat, acc, jnp.zeros((groups, feat, dh), F32), jnp.zeros((groups, 8, feat), F32)]
    mine = local(queries, own, query_map, key_map, pair)
    blocks, flags, sigs = [], [], []
    for i in range(1, outer + 1):
        now = (along[i : i + 1] if i < outer else []) + across[i - 1]
        if now:
            here = [b for b, _ in now]
            on = jnp.stack([f.astype(jnp.int32) for _, f in now])
            *state, sig = attend(turned, here, on, key_map, state, heads, 4)
            sigs.append(sig)
            blocks += here
            flags.append(on)
    flags = jnp.concatenate(flags)

    total_heads = heads * lax.axis_size("head")
    cells = (total_heads + groups * lax.axis_size("head")) * dh * feat
    places = jnp.stack([outer_me, inner_me]).astype(jnp.int32)
    scalars = jnp.concatenate([flags, places])
    share = (ratio + 1) * dh // total
    sizes = (groups, heads, outer, inner, dh, feat)
    over = lambda d: [(at(p, j), at(p, (j + d) % inner)) for p in range(outer) for j in range(inner)]
    up = lambda d: [(at(p, j), at((p + d) % outer, j)) for p in range(outer) for j in range(inner)]
    vmem = pl.BlockSpec(memory_space=pltpu.VMEM)
    lines = []
    for g in range(groups):
        parts = learn(g, scalars, queries, own, state, mine, blocks, sigs, sizes, pair)
        taken = [lax.ppermute(parts[d], "seq", over(d)) for d in range(1, inner)]
        half = [functools.reduce(jnp.add, [x[f] for x in taken], parts[0][f]) for f in range(outer)]
        taken = [lax.ppermute(half[d], "seq", up(d)) for d in range(1, outer)]
        piece = pl.pallas_call(
            piece_kernel,
            out_shape=jax.ShapeDtypeStruct((share + 8, feat), F32),
            in_specs=[vmem] * outer,
            out_specs=vmem,
            compiler_params=pltpu.CompilerParams(vmem_limit_bytes=LIMIT),
            name=f"piece{g}",
        )(half[0], *taken)
        found = [piece] + [lax.ppermute(piece, "seq", up(d)) for d in range(1, outer)]
        lines.append(jnp.stack(found))

    squares = sum(x[f, share:] for x in lines for f in range(outer))
    squares = squares + sum(lax.ppermute(squares, "seq", over(d)) for d in range(1, inner)) if inner > 1 else squares
    squares = butterfly(squares, "head")
    crossed = [[line] + [lax.ppermute(line, "seq", over(d)) for d in range(1, inner)] for line in lines]
    crossed = [x for group in crossed for x in group]
    q_rows, k_rows = ratio * dh // total, dh // total
    gq, gk = pl.pallas_call(
        functools.partial(finish_kernel, groups, inner, outer, q_rows, k_rows, cells),
        out_shape=[
            jax.ShapeDtypeStruct((heads * dh, feat), F32),
            jax.ShapeDtypeStruct((groups * dh, feat), F32),
        ],
        in_specs=[pl.BlockSpec(memory_space=pltpu.SMEM)] + [vmem] * (1 + len(crossed)),
        compiler_params=pltpu.CompilerParams(vmem_limit_bytes=LIMIT),
        name="finish",
    )(places, squares, *crossed)
    return gq.reshape(heads, dh, feat), gk.reshape(groups, dh, feat)


def solution(mesh):
    placed = (
        P("seq", "head"),
        P("seq", "head"),
        P("seq", "head"),
        P("head", None, None),
        P("head", None, None),
    )
    return jax.shard_map(
        on_device,
        mesh=mesh,
        in_specs=placed,
        out_specs=(P("head", None, None), P("head", None, None)),
        check_vma=False,
    )
```

```python
import functools
import math

import jax
import jax.numpy as jnp
from jax import lax
from jax.experimental import pallas as pl
from jax.experimental.pallas import tpu as pltpu
from jax.sharding import PartitionSpec as P


EPSILON = 1e-06
F32 = jnp.float32
BF16 = jnp.bfloat16
LIMIT = 20 * 2**20
NN = (((1,), (0,)), ((), ()))
TN = (((0,), (0,)), ((), ()))


def split(x):
    hi = x.astype(BF16)
    lo = (x - hi.astype(F32)).astype(BF16)
    return hi, lo


def mm(a, b, dims=NN):
    return lax.dot_general(a, b, dims, preferred_element_type=F32)


def wide(x):
    return jnp.concatenate(split(x), axis=1)


def tall(hi):
    return jnp.concatenate([hi, hi], axis=0)


def fold(x):
    half = x.shape[1] // 2
    return x[:, :half] + x[:, half:]


def square(x):
    return tall(wide(x))


def softplus(x):
    return jnp.maximum(x, 0.0) + jnp.log1p(jnp.exp(-jnp.abs(x)))


def sigmoid(x):
    e = jnp.exp(-jnp.abs(x))
    r = 1.0 / (1.0 + e)
    return jnp.where(x >= 0.0, r, e * r)


def row_sum(x):
    return jnp.sum(x, axis=1, keepdims=True)


def attend_kernel(first, count, groups, pair, scale, flags, *refs):
    q_ref = refs[0]
    blocks = refs[1 : 1 + count]
    if first:
        qt_ref, stat_out, acc_out = refs[1 + count : 4 + count]
        keys, vals = refs[4 + count :]
    else:
        wk_ref, _, _, _, _ = refs[1 + count : 6 + count]
        stat_out, acc_out, st_out, nm_out, sig_out = refs[6 + count : 11 + count]
        keys, vals = refs[11 + count :]
    rows = blocks[0].shape[0]
    dh = blocks[0].shape[1] // (2 * groups)
    heads = acc_out.shape[0]
    steps = heads // groups // pair
    on = flags[0]
    for b in range(1, count):
        on = on + flags[b]

    def prepare(b):
        for g in range(groups):
            value = blocks[b][:, (groups + g) * dh : (groups + g + 1) * dh]
            key_wide = wide(blocks[b][:, g * dh : (g + 1) * dh])
            keys[g, b * rows : (b + 1) * rows, :] = key_wide
            vals[g, :, b * rows : (b + 1) * rows] = jnp.concatenate(split(value.T), axis=0)
            if not first:
                act = fold(mm(key_wide, square(wk_ref[g])))
                sig_out[b, g] = sigmoid(act)
                feat = softplus(act)
                fh, fl = split(feat)
                val_wide = wide(value)
                st_out[g] += fold(mm(fh, val_wide, TN)) + mm(fl, val_wide[:, :dh], TN)
                nm_out[g] += jnp.sum(feat.reshape(-1, 8, feat.shape[1]), axis=0)

    def update(begin, number):
        def some_heads(j, _):
            g = lax.div(j, steps)

            def scores(p):
                h = j * pair + p
                if first:
                    q = q_ref[:, pl.ds(pl.multiple_of(h * dh, dh), dh)] * scale
                    q_t = jnp.concatenate(split(q.T), axis=0)
                    qt_ref[h] = q_t
                else:
                    q_t = q_ref[h]
                q_hi, q_lo = tall(q_t[:dh]), q_t[dh:]
                found = []
                for b in range(number):
                    key = keys[g, (begin + b) * rows : (begin + b + 1) * rows, :]
                    s = mm(key, q_hi) + mm(key[:, :dh], q_lo)
                    if first:
                        before = lax.broadcasted_iota(jnp.int32, s.shape, 0) <= lax.broadcasted_iota(jnp.int32, s.shape, 1)
                        s = jnp.where(before, s, -1e30)
                    found.append(s)
                return found

            ahead = scores(0)
            for p in range(pair):
                h = j * pair + p
                now = ahead
                new = functools.reduce(jnp.maximum, [jnp.max(s, axis=0, keepdims=True) for s in now])
                if not first:
                    old = stat_out[h, 0:1, :]
                    new = jnp.maximum(old, new)
                    fade = jnp.exp2(old - new)
                if p + 1 < pair:
                    ahead = scores(p + 1)
                tot, out = 0.0, 0.0
                for b in range(number):
                    w = jnp.exp2(now[b] - new)
                    tot = tot + jnp.sum(w, axis=0, keepdims=True)
                    wh, wl = split(w)
                    val = vals[g, :, (begin + b) * rows : (begin + b + 1) * rows]
                    both = mm(val, wh)
                    out = out + both[:dh] + both[dh:] + mm(val[:dh], wl)
                if not first:
                    tot = tot + fade * stat_out[h, 1:2, :]
                    out = out + fade * acc_out[h]
                stat_out[h, 0:1, :] = new
                stat_out[h, 1:2, :] = tot
                acc_out[h] = out
            return 0

        lax.fori_loop(0, heads // pair, some_heads, 0)

    if first:
        prepare(0)
        update(0, 1)
        return

    @pl.when(on == count)
    def _():
        for b in range(count):
            prepare(b)
        update(0, count)

    if count > 1:
        for b in range(count):

            @pl.when(jnp.logical_and(on < count, flags[b] > 0))
            def _():
                prepare(b)
                update(b, 1)


def attend(q, blocks, flags, key_map, state, heads, pair):
    groups, dh, feat = key_map.shape
    rows = blocks[0].shape[0]
    count = len(blocks)
    first = state is None
    tokens = rows if first else q.shape[2]
    stat_shape = jax.ShapeDtypeStruct((heads, 2, tokens), F32)
    acc_shape = jax.ShapeDtypeStruct((heads, dh, tokens), F32)
    vmem = pl.BlockSpec(memory_space=pltpu.VMEM)
    smem = pl.BlockSpec(memory_space=pltpu.SMEM)
    alias = {}
    if first:
        args = [q, *blocks]
        out_shape = [jax.ShapeDtypeStruct((heads, 2 * dh, rows), BF16), stat_shape, acc_shape]
    else:
        args = [q, *blocks, key_map, *state]
        out_shape = [
            stat_shape,
            acc_shape,
            jax.ShapeDtypeStruct((groups, feat, dh), F32),
            jax.ShapeDtypeStruct((groups, 8, feat), F32),
            jax.ShapeDtypeStruct((count, groups, rows, feat), F32),
        ]
        alias = {3 + count + i: i for i in range(4)}
    scale = math.log2(math.e) * dh ** (-0.5)
    return pl.pallas_call(
        functools.partial(attend_kernel, first, count, groups, pair, scale),
        out_shape=out_shape,
        in_specs=[smem] + [vmem] * len(args),
        out_specs=[vmem] * len(out_shape),
        scratch_shapes=[
            pltpu.VMEM((groups, count * rows, 2 * dh), BF16),
            pltpu.VMEM((groups, 2 * dh, count * rows), BF16),
        ],
        input_output_aliases=alias,
        compiler_params=pltpu.CompilerParams(vmem_limit_bytes=LIMIT),
        cost_estimate=pl.CostEstimate(
            flops=heads * count * 24 * rows * tokens * dh,
            bytes_accessed=4 * tokens * dh * heads * 3,
            transcendentals=heads * count * rows * tokens,
        ),
        name="attend",
    )(flags, *args)


def causal_mask(rows):
    return lax.broadcasted_iota(jnp.int32, (rows, rows), 0) >= lax.broadcasted_iota(jnp.int32, (rows, rows), 1)


def local_kernel(groups, pair, *refs):
    q_ref, kv_ref, wq_ref, wk_ref, qf_ref, sig_ref, num_ref, part_ref, feat_ref, sig_k_ref, turned, turned_lo, val_w = refs
    heads, dh, feat_dim = wq_ref.shape
    rows = q_ref.shape[0]
    steps = heads // groups // pair
    for g in range(groups):
        act = fold(mm(wide(kv_ref[:, g * dh : (g + 1) * dh]), square(wk_ref[g])))
        feat = softplus(act)
        sig_k_ref[g] = sigmoid(act)
        hi, lo = split(feat.T)
        turned[g] = tall(hi)
        turned_lo[g] = lo
        feat_ref[g] = wide(feat)
        val_w[g] = wide(kv_ref[:, (groups + g) * dh : (groups + g + 1) * dh])
    causal = causal_mask(rows)

    def some_heads(j, _):
        g = lax.div(j, steps)
        each = [j * pair + p for p in range(pair)]
        q = [wide(q_ref[:, pl.ds(pl.multiple_of(h * dh, dh), dh)]) for h in each]
        act = [fold(mm(x, square(wq_ref[h]))) for x, h in zip(q, each)]
        qf = [wide(softplus(x)) for x in act]
        for x, y, h in zip(act, qf, each):
            sig_ref[h] = sigmoid(x)
            qf_ref[h] = y
        kern = [mm(x, turned[g]) + mm(x[:, :feat_dim], turned_lo[g]) for x in qf]
        kern = [jnp.where(causal, x, 0.0) for x in kern]
        for x, h in zip(kern, each):
            part_ref[h] = functools.reduce(
                jnp.add, [x[:, c : c + feat_dim] for c in range(0, rows, feat_dim)]
            )
        halves = [split(x) for x in kern]
        val = val_w[g]
        for (hi, lo), h in zip(halves, each):
            num_ref[h] = fold(mm(hi, val)) + mm(lo, val[:, :dh])
        return 0

    lax.fori_loop(0, heads // pair, some_heads, 0)


def vmem_call(kernel, args, out_shape, scratch, flops, first_smem=True):
    vmem = pl.BlockSpec(memory_space=pltpu.VMEM)
    smem = pl.BlockSpec(memory_space=pltpu.SMEM)
    return pl.pallas_call(
        kernel,
        out_shape=out_shape,
        in_specs=([smem] if first_smem else [vmem]) + [vmem] * (len(args) - 1),
        out_specs=[vmem] * len(out_shape),
        scratch_shapes=scratch,
        compiler_params=pltpu.CompilerParams(vmem_limit_bytes=LIMIT),
        cost_estimate=pl.CostEstimate(flops=flops, bytes_accessed=2**22, transcendentals=2**20),
    )(*args)


def local(q, own, query_map, key_map, pair):
    heads, dh, feat = query_map.shape
    groups = key_map.shape[0]
    rows = q.shape[0]
    shape = jax.ShapeDtypeStruct
    return vmem_call(
        functools.partial(local_kernel, groups, pair),
        [q, own, query_map, key_map],
        [
            shape((heads, rows, 2 * feat), BF16),
            shape((heads, rows, feat), F32),
            shape((heads, rows, dh), F32),
            shape((heads, rows, feat), F32),
            shape((groups, rows, 2 * feat), BF16),
            shape((groups, rows, feat), F32),
        ],
        [
            pltpu.VMEM((groups, 2 * feat, rows), BF16),
            pltpu.VMEM((groups, feat, rows), BF16),
            pltpu.VMEM((groups, rows, 2 * dh), BF16),
        ],
        heads * 24 * rows * rows * dh,
        first_smem=False,
    )


def learn_kernel(group, groups, counts, pair, outer, inner, flags, *refs):
    count = sum(counts)
    q_ref, kv_ref, st_ref, nm_ref, stat_ref, acc_ref = refs[:6]
    qf_ref, sig_ref, num_ref, part_ref, feat_ref, sig_k_ref = refs[6:12]
    blocks = refs[12 : 12 + count]
    sigs = refs[12 + count : 12 + count + len(counts)]
    outs = refs[12 + count + len(counts) : 12 + count + len(counts) + inner]
    val_t2, val_t_lo, st_sq, st_t_sq, adj, adj_n, result = refs[12 + count + len(counts) + inner :]
    heads, rows, dh = num_ref.shape
    feat_dim = sig_ref.shape[2]
    ratio = heads // groups
    total = outer * inner
    q_rows, k_rows = ratio * dh // total, dh // total
    outer_me, inner_me = flags[count], flags[count + 1]
    columns = slice(group * dh, (group + 1) * dh)
    val_columns = slice((groups + group) * dh, (groups + group + 1) * dh)

    def place(s):
        i, j = lax.div(s, inner), lax.rem(s, inner)
        return lax.rem(j - inner_me + inner, inner), lax.rem(i - outer_me + outer, outer)

    hi, lo = split(kv_ref[:, val_columns].T)
    val_t2[...] = tall(hi)
    val_t_lo[...] = lo
    st_sq[...] = square(st_ref[group])
    st_t_sq[...] = square(st_ref[group].T)
    adj[...] = jnp.zeros_like(adj)
    adj_n[...] = jnp.zeros_like(adj_n)
    norm_prev = jnp.sum(nm_ref[group], axis=0, keepdims=True)
    causal = causal_mask(rows)

    def some_heads(j, _):
        each = [group * ratio + j * pair + p for p in range(pair)]
        teacher = [(acc_ref[h] / stat_ref[h, 1:2, :]).T for h in each]
        qfw = [qf_ref[h] for h in each]
        qf = [x[:, :feat_dim].astype(F32) + x[:, feat_dim:].astype(F32) for x in qfw]
        num = [num_ref[h] + fold(mm(x, st_sq[...])) for x, h in zip(qfw, each)]
        inv = [1.0 / row_sum(part_ref[h] + x * norm_prev) for x, h in zip(qf, each)]
        student = [x * y for x, y in zip(num, inv)]
        mismatch = [x - y for x, y in zip(student, teacher)]
        gn = [wide(x * y) for x, y in zip(mismatch, inv)]
        gd = [-row_sum(x * y) * z for x, y, z in zip(mismatch, student, inv)]
        coupling = [mm(x, val_t2[...]) + mm(x[:, :dh], val_t_lo[...]) for x in gn]
        coupling = [split(jnp.where(causal, x + y, 0.0)) for x, y in zip(coupling, gd)]
        feat = feat_ref[group]
        gqf = [
            fold(mm(hi, feat)) + mm(lo, feat[:, :feat_dim]) + fold(mm(x, st_t_sq[...])) + y * norm_prev
            for (hi, lo), x, y in zip(coupling, gn, gd)
        ]
        for (hi, lo), x, y in zip(coupling, gn, qfw):
            left_hi = jnp.concatenate([hi, x[:, :dh]], axis=1)
            left_lo = jnp.concatenate([lo, x[:, dh:]], axis=1)
            adj[...] += fold(mm(left_hi, y, TN)) + mm(left_lo, y[:, :feat_dim], TN)
        for x, y in zip(qf, gd):
            adj_n[...] += jnp.sum((x * y).reshape(-1, 8, feat_dim), axis=0)
        back = [wide(x * sig_ref[h]) for x, h in zip(gqf, each)]
        for p, (x, h) in enumerate(zip(back, each)):
            hi, lo = split(q_ref[:, pl.ds(pl.multiple_of(h * dh, dh), dh)])
            grad = fold(mm(hi, x, TN)) + mm(lo, x[:, :feat_dim], TN)
            first = (j * pair + p) * (dh // q_rows)
            for k in range(dh // q_rows):
                e, f = place(first + k)
                result[e, f, :q_rows, :] = grad[k * q_rows : (k + 1) * q_rows]
        return 0

    lax.fori_loop(0, ratio // pair, some_heads, 0)

    def key_side(keys, x):
        xw = wide(x)
        hi, lo = split(keys)
        return fold(mm(hi, xw, TN)) + mm(lo, xw[:, :feat_dim], TN)

    adj_sq = square(adj[rows:])
    adj_norm = jnp.sum(adj_n[...], axis=0, keepdims=True)
    grad_k = key_side(kv_ref[:, columns], adj[:rows] * sig_k_ref[group])
    b = 0
    for stage, number in enumerate(counts):
        for k in range(number):
            grad = fold(mm(wide(blocks[b][:, val_columns]), adj_sq)) + adj_norm
            more = key_side(blocks[b][:, columns], grad * sigs[stage][k, group])
            grad_k = grad_k + jnp.where(flags[b] > 0, more, 0.0)
            b += 1
    for s in range(total):
        e, f = place(s)
        result[e, f, q_rows:, :] = grad_k[s * k_rows : (s + 1) * k_rows]
    for e in range(inner):
        outs[e][...] = result[e]


def learn(group, flags, q, own, state, mine, blocks, sigs, sizes, pair):
    groups, heads, outer, inner, dh, feat = sizes
    rows = own.shape[0]
    total = outer * inner
    share = (heads // groups + 1) * dh // total
    counts = tuple(x.shape[0] for x in sigs)
    stat, acc, st, nm = state
    args = [flags, q, own, st, nm, stat, acc, *mine, *blocks, *sigs]
    return vmem_call(
        functools.partial(learn_kernel, group, groups, counts, pair, outer, inner),
        args,
        [jax.ShapeDtypeStruct((outer, share, feat), F32)] * inner,
        [
            pltpu.VMEM((2 * dh, rows), BF16),
            pltpu.VMEM((dh, rows), BF16),
            pltpu.VMEM((2 * feat, 2 * dh), BF16),
            pltpu.VMEM((2 * dh, 2 * feat), BF16),
            pltpu.VMEM((rows + dh, feat), F32),
            pltpu.VMEM((8, feat), F32),
            pltpu.VMEM((inner, outer, share, feat), F32),
        ],
        heads // groups * 40 * rows * rows * dh,
    )


def pack_kernel(k_ref, v_ref, out_ref):
    width = k_ref.shape[1]
    out_ref[:, :width] = k_ref[...]
    out_ref[:, width:] = v_ref[...]


def piece_kernel(*refs):
    out = refs[-1]
    rows = refs[0].shape[0]
    value = functools.reduce(jnp.add, [r[...] for r in refs[:-1]])
    out[:rows, :] = value
    squares = jnp.sum((value * value).reshape(-1, 8, value.shape[1]), axis=0)
    out[rows:, :] = squares


def finish_kernel(groups, inner, outer, q_rows, k_rows, count, where, *refs):
    squares = refs[0]
    lines = refs[1 : 1 + groups * inner]
    gq_ref, gk_ref = refs[1 + groups * inner :]
    mean = jnp.sum(jnp.sum(squares[...], axis=0, keepdims=True), axis=1, keepdims=True) / count
    factor = 1.0 / jnp.sqrt(mean + EPSILON)
    total = outer * inner
    for g in range(groups):
        for e in range(inner):
            for f in range(outer):
                i = lax.rem(where[0] - f + outer, outer)
                j = lax.rem(where[1] - e + inner, inner)
                s = i * inner + j
                line = lines[g * inner + e]
                q_at = pl.multiple_of((g * total + s) * q_rows, q_rows)
                k_at = pl.multiple_of((g * total + s) * k_rows, k_rows)
                gq_ref[pl.ds(q_at, q_rows), :] = line[f, :q_rows, :] * factor
                gk_ref[pl.ds(k_at, k_rows), :] = line[f, q_rows : q_rows + k_rows, :] * factor


def butterfly(value, axis):
    size = lax.axis_size(axis)
    hop = 1
    while hop < size:
        value = value + ppermute(value, [(s, s ^ hop) for s in range(size)], axis)
        hop *= 2
    return value


def ppermute(value, pairs, axis="seq"):
    return lax.ppermute(value, axis, pairs)


def on_device(queries, key_heads, value_heads, query_map, key_map):
    heads = query_map.shape[0]
    groups, dh, feat = key_map.shape
    rows = queries.shape[0]
    ratio = heads // groups
    pair = 2 if ratio % 2 == 0 else 1
    total = lax.axis_size("seq")
    inner = 1 << ((total.bit_length() - 1) // 2)
    outer = total // inner
    me = lax.axis_index("seq")
    outer_me, inner_me = me // inner, me % inner
    at = lambda i, j: i * inner + j
    own = pl.pallas_call(
        pack_kernel,
        out_shape=jax.ShapeDtypeStruct((rows, 2 * groups * dh), F32),
        out_specs=pl.BlockSpec(memory_space=pltpu.VMEM),
        compiler_params=pltpu.CompilerParams(vmem_limit_bytes=LIMIT),
        name="pack",
    )(key_heads, value_heads)

    along, across = [], []
    moving = own
    for i in range(outer):
        if i > 0:
            pairs = [(at(p, j), at(p + 1, j)) for p in range(i - 1, outer - 1) for j in range(inner)]
            moving = ppermute(moving, pairs)
        along.append((moving, outer_me >= i))
        side = []
        last = i == outer - 1 and i > 0
        for d in range(1, inner):
            pairs = [
                (at(p, (j + d) % inner), at(p, j))
                for p in range(i, outer)
                for j in range(inner)
                if i > 0 or (j + d) % inner < j
            ]
            flag = outer_me >= i if i > 0 else (inner_me + d) % inner < inner_me
            if last and rows % 16 == 0:
                half = rows // 2
                ahead = across[i - 1][d - 1][0]
                line = [(at(i - 1, j), at(i, j)) for j in range(inner)]
                parts = [ppermute(moving[:half], pairs), ppermute(ahead[half:], line)]
                side.append((jnp.concatenate(parts, axis=0), flag))
            else:
                side.append((ppermute(moving, pairs), flag))
        across.append(side)

    always = jnp.ones((1,), jnp.int32)
    turned, stat, acc = attend(queries, [own], always, key_map, None, heads, 4)
    state = [stat, acc, jnp.zeros((groups, feat, dh), F32), jnp.zeros((groups, 8, feat), F32)]
    mine = local(queries, own, query_map, key_map, pair)
    blocks, flags, sigs = [], [], []
    for i in range(1, outer + 1):
        now = (along[i : i + 1] if i < outer else []) + across[i - 1]
        if now:
            here = [b for b, _ in now]
            on = jnp.stack([f.astype(jnp.int32) for _, f in now])
            *state, sig = attend(turned, here, on, key_map, state, heads, 4)
            sigs.append(sig)
            blocks += here
            flags.append(on)
    flags = jnp.concatenate(flags)

    total_heads = heads * lax.axis_size("head")
    cells = (total_heads + groups * lax.axis_size("head")) * dh * feat
    places = jnp.stack([outer_me, inner_me]).astype(jnp.int32)
    scalars = jnp.concatenate([flags, places])
    share = (ratio + 1) * dh // total
    sizes = (groups, heads, outer, inner, dh, feat)
    over = lambda d: [(at(p, j), at(p, (j + d) % inner)) for p in range(outer) for j in range(inner)]
    up = lambda d: [(at(p, j), at((p + d) % outer, j)) for p in range(outer) for j in range(inner)]
    vmem = pl.BlockSpec(memory_space=pltpu.VMEM)
    lines = []
    for g in range(groups):
        parts = learn(g, scalars, queries, own, state, mine, blocks, sigs, sizes, pair)
        taken = [ppermute(parts[d], over(d)) for d in range(1, inner)]
        half = [functools.reduce(jnp.add, [x[f] for x in taken], parts[0][f]) for f in range(outer)]
        taken = [ppermute(half[d], up(d)) for d in range(1, outer)]
        piece = pl.pallas_call(
            piece_kernel,
            out_shape=jax.ShapeDtypeStruct((share + 8, feat), F32),
            in_specs=[vmem] * outer,
            out_specs=vmem,
            compiler_params=pltpu.CompilerParams(vmem_limit_bytes=LIMIT),
        )(half[0], *taken)
        found = [piece] + [ppermute(piece, up(d)) for d in range(1, outer)]
        lines.append(jnp.stack(found))

    squares = sum(x[f, share:] for x in lines for f in range(outer))
    squares = butterfly(squares, "head")
    squares = functools.reduce(jnp.add, [ppermute(squares, over(d)) for d in range(1, inner)], squares)
    crossed = [[line] + [ppermute(line, over(d)) for d in range(1, inner)] for line in lines]
    crossed = [x for group in crossed for x in group]
    q_rows, k_rows = ratio * dh // total, dh // total
    gq, gk = pl.pallas_call(
        functools.partial(finish_kernel, groups, inner, outer, q_rows, k_rows, cells),
        out_shape=[
            jax.ShapeDtypeStruct((heads * dh, feat), F32),
            jax.ShapeDtypeStruct((groups * dh, feat), F32),
        ],
        in_specs=[pl.BlockSpec(memory_space=pltpu.SMEM)] + [vmem] * (1 + len(crossed)),
        compiler_params=pltpu.CompilerParams(vmem_limit_bytes=LIMIT),
        name="finish",
    )(places, squares, *crossed)
    return gq.reshape(heads, dh, feat), gk.reshape(groups, dh, feat)


def solution(mesh):
    placed = (
        P("seq", "head"),
        P("seq", "head"),
        P("seq", "head"),
        P("head", None, None),
        P("head", None, None),
    )

    return jax.shard_map(
        on_device,
        mesh=mesh,
        in_specs=placed,
        out_specs=(P("head", None, None), P("head", None, None)),
        check_vma=False,
    )
```

```python
import functools
import math

import jax
import jax.numpy as jnp
from jax import lax
from jax.experimental import pallas as pl
from jax.experimental.pallas import tpu as pltpu
from jax.sharding import PartitionSpec as P


EPSILON = 1e-06
F32 = jnp.float32
BF16 = jnp.bfloat16
LIMIT = 20 * 2**20
NN = (((1,), (0,)), ((), ()))
TN = (((0,), (0,)), ((), ()))


def split(x):
    hi = x.astype(BF16)
    lo = (x - hi.astype(F32)).astype(BF16)
    return hi, lo


def mm(a, b, dims=NN):
    return lax.dot_general(a, b, dims, preferred_element_type=F32)


def wide(x):
    return jnp.concatenate(split(x), axis=1)


def tall(hi):
    return jnp.concatenate([hi, hi], axis=0)


def fold(x):
    half = x.shape[1] // 2
    return x[:, :half] + x[:, half:]


def square(x):
    return tall(wide(x))


def softplus(x):
    return jnp.maximum(x, 0.0) + jnp.log1p(jnp.exp(-jnp.abs(x)))


def sigmoid(x):
    e = jnp.exp(-jnp.abs(x))
    r = 1.0 / (1.0 + e)
    return jnp.where(x >= 0.0, r, e * r)


def row_sum(x):
    return jnp.sum(x, axis=1, keepdims=True)


def attend_kernel(first, count, groups, pair, scale, flags, *refs):
    q_ref = refs[0]
    blocks = refs[1 : 1 + count]
    if first:
        qt_ref, stat_out, acc_out = refs[1 + count : 4 + count]
        keys, vals = refs[4 + count :]
    else:
        wk_ref, _, _, _, _ = refs[1 + count : 6 + count]
        stat_out, acc_out, st_out, nm_out, sig_out = refs[6 + count : 11 + count]
        keys, vals = refs[11 + count :]
    rows = blocks[0].shape[0]
    dh = blocks[0].shape[1] // (2 * groups)
    heads = acc_out.shape[0]
    steps = heads // groups // pair
    on = flags[0]
    for b in range(1, count):
        on = on + flags[b]

    def prepare(b):
        for g in range(groups):
            value = blocks[b][:, (groups + g) * dh : (groups + g + 1) * dh]
            key_wide = wide(blocks[b][:, g * dh : (g + 1) * dh])
            keys[g, b * rows : (b + 1) * rows, :] = key_wide
            vals[g, :, b * rows : (b + 1) * rows] = jnp.concatenate(split(value.T), axis=0)
            if not first:
                act = fold(mm(key_wide, square(wk_ref[g])))
                sig_out[b, g] = sigmoid(act)
                feat = softplus(act)
                fh, fl = split(feat)
                val_wide = wide(value)
                st_out[g] += fold(mm(fh, val_wide, TN)) + mm(fl, val_wide[:, :dh], TN)
                nm_out[g] += jnp.sum(feat.reshape(-1, 8, feat.shape[1]), axis=0)

    def update(begin, number):
        def some_heads(j, _):
            g = lax.div(j, steps)

            def scores(p):
                h = j * pair + p
                if first:
                    q = q_ref[:, pl.ds(pl.multiple_of(h * dh, dh), dh)] * scale
                    q_t = jnp.concatenate(split(q.T), axis=0)
                    qt_ref[h] = q_t
                else:
                    q_t = q_ref[h]
                q_hi, q_lo = tall(q_t[:dh]), q_t[dh:]
                found = []
                for b in range(number):
                    key = keys[g, (begin + b) * rows : (begin + b + 1) * rows, :]
                    s = mm(key, q_hi) + mm(key[:, :dh], q_lo)
                    if first:
                        before = lax.broadcasted_iota(jnp.int32, s.shape, 0) <= lax.broadcasted_iota(jnp.int32, s.shape, 1)
                        s = jnp.where(before, s, -1e30)
                    found.append(s)
                return found

            ahead = scores(0)
            for p in range(pair):
                h = j * pair + p
                now = ahead
                new = functools.reduce(jnp.maximum, [jnp.max(s, axis=0, keepdims=True) for s in now])
                if not first:
                    old = stat_out[h, 0:1, :]
                    new = jnp.maximum(old, new)
                    fade = jnp.exp2(old - new)
                if p + 1 < pair:
                    ahead = scores(p + 1)
                tot, out = 0.0, 0.0
                for b in range(number):
                    w = jnp.exp2(now[b] - new)
                    tot = tot + jnp.sum(w, axis=0, keepdims=True)
                    wh, wl = split(w)
                    val = vals[g, :, (begin + b) * rows : (begin + b + 1) * rows]
                    both = mm(val, wh)
                    out = out + both[:dh] + both[dh:] + mm(val[:dh], wl)
                if not first:
                    tot = tot + fade * stat_out[h, 1:2, :]
                    out = out + fade * acc_out[h]
                stat_out[h, 0:1, :] = new
                stat_out[h, 1:2, :] = tot
                acc_out[h] = out
            return 0

        lax.fori_loop(0, heads // pair, some_heads, 0)

    if first:
        prepare(0)
        update(0, 1)
        return

    @pl.when(on == count)
    def _():
        for b in range(count):
            prepare(b)
        update(0, count)

    if count > 1:
        for b in range(count):

            @pl.when(jnp.logical_and(on < count, flags[b] > 0))
            def _():
                prepare(b)
                update(b, 1)


def attend(q, blocks, flags, key_map, state, heads, pair):
    groups, dh, feat = key_map.shape
    rows = blocks[0].shape[0]
    count = len(blocks)
    first = state is None
    tokens = rows if first else q.shape[2]
    stat_shape = jax.ShapeDtypeStruct((heads, 2, tokens), F32)
    acc_shape = jax.ShapeDtypeStruct((heads, dh, tokens), F32)
    vmem = pl.BlockSpec(memory_space=pltpu.VMEM)
    smem = pl.BlockSpec(memory_space=pltpu.SMEM)
    alias = {}
    if first:
        args = [q, *blocks]
        out_shape = [jax.ShapeDtypeStruct((heads, 2 * dh, rows), BF16), stat_shape, acc_shape]
    else:
        args = [q, *blocks, key_map, *state]
        out_shape = [
            stat_shape,
            acc_shape,
            jax.ShapeDtypeStruct((groups, feat, dh), F32),
            jax.ShapeDtypeStruct((groups, 8, feat), F32),
            jax.ShapeDtypeStruct((count, groups, rows, feat), F32),
        ]
        alias = {3 + count + i: i for i in range(4)}
    scale = math.log2(math.e) * dh ** (-0.5)
    return pl.pallas_call(
        functools.partial(attend_kernel, first, count, groups, pair, scale),
        out_shape=out_shape,
        in_specs=[smem] + [vmem] * len(args),
        out_specs=[vmem] * len(out_shape),
        scratch_shapes=[
            pltpu.VMEM((groups, count * rows, 2 * dh), BF16),
            pltpu.VMEM((groups, 2 * dh, count * rows), BF16),
        ],
        input_output_aliases=alias,
        compiler_params=pltpu.CompilerParams(vmem_limit_bytes=LIMIT),
        cost_estimate=pl.CostEstimate(
            flops=heads * count * 24 * rows * tokens * dh,
            bytes_accessed=4 * tokens * dh * heads * 3,
            transcendentals=heads * count * rows * tokens,
        ),
        name="attend",
    )(flags, *args)


def causal_mask(rows):
    return lax.broadcasted_iota(jnp.int32, (rows, rows), 0) >= lax.broadcasted_iota(jnp.int32, (rows, rows), 1)


def local_kernel(groups, pair, *refs):
    q_ref, kv_ref, wq_ref, wk_ref, qf_ref, sig_ref, num_ref, part_ref, feat_ref, sig_k_ref, turned, turned_lo, val_w = refs
    heads, dh, feat_dim = wq_ref.shape
    rows = q_ref.shape[0]
    steps = heads // groups // pair
    for g in range(groups):
        act = fold(mm(wide(kv_ref[:, g * dh : (g + 1) * dh]), square(wk_ref[g])))
        feat = softplus(act)
        sig_k_ref[g] = sigmoid(act)
        hi, lo = split(feat.T)
        turned[g] = tall(hi)
        turned_lo[g] = lo
        feat_ref[g] = wide(feat)
        val_w[g] = wide(kv_ref[:, (groups + g) * dh : (groups + g + 1) * dh])
    causal = causal_mask(rows)

    def some_heads(j, _):
        g = lax.div(j, steps)
        each = [j * pair + p for p in range(pair)]
        q = [wide(q_ref[:, pl.ds(pl.multiple_of(h * dh, dh), dh)]) for h in each]
        act = [fold(mm(x, square(wq_ref[h]))) for x, h in zip(q, each)]
        qf = [wide(softplus(x)) for x in act]
        for x, y, h in zip(act, qf, each):
            sig_ref[h] = sigmoid(x)
            qf_ref[h] = y
        kern = [mm(x, turned[g]) + mm(x[:, :feat_dim], turned_lo[g]) for x in qf]
        kern = [jnp.where(causal, x, 0.0) for x in kern]
        for x, h in zip(kern, each):
            part_ref[h] = functools.reduce(
                jnp.add, [x[:, c : c + feat_dim] for c in range(0, rows, feat_dim)]
            )
        halves = [split(x) for x in kern]
        val = val_w[g]
        for (hi, lo), h in zip(halves, each):
            num_ref[h] = fold(mm(hi, val)) + mm(lo, val[:, :dh])
        return 0

    lax.fori_loop(0, heads // pair, some_heads, 0)


def vmem_call(kernel, args, out_shape, scratch, flops, first_smem=True):
    vmem = pl.BlockSpec(memory_space=pltpu.VMEM)
    smem = pl.BlockSpec(memory_space=pltpu.SMEM)
    return pl.pallas_call(
        kernel,
        out_shape=out_shape,
        in_specs=([smem] if first_smem else [vmem]) + [vmem] * (len(args) - 1),
        out_specs=[vmem] * len(out_shape),
        scratch_shapes=scratch,
        compiler_params=pltpu.CompilerParams(vmem_limit_bytes=LIMIT),
        cost_estimate=pl.CostEstimate(flops=flops, bytes_accessed=2**22, transcendentals=2**20),
    )(*args)


def local(q, own, query_map, key_map, pair):
    heads, dh, feat = query_map.shape
    groups = key_map.shape[0]
    rows = q.shape[0]
    shape = jax.ShapeDtypeStruct
    return vmem_call(
        functools.partial(local_kernel, groups, pair),
        [q, own, query_map, key_map],
        [
            shape((heads, rows, 2 * feat), BF16),
            shape((heads, rows, feat), F32),
            shape((heads, rows, dh), F32),
            shape((heads, rows, feat), F32),
            shape((groups, rows, 2 * feat), BF16),
            shape((groups, rows, feat), F32),
        ],
        [
            pltpu.VMEM((groups, 2 * feat, rows), BF16),
            pltpu.VMEM((groups, feat, rows), BF16),
            pltpu.VMEM((groups, rows, 2 * dh), BF16),
        ],
        heads * 24 * rows * rows * dh,
        first_smem=False,
    )


def learn_kernel(group, groups, counts, pair, outer, inner, flags, *refs):
    count = sum(counts)
    q_ref, kv_ref, st_ref, nm_ref, stat_ref, acc_ref = refs[:6]
    qf_ref, sig_ref, num_ref, part_ref, feat_ref, sig_k_ref = refs[6:12]
    blocks = refs[12 : 12 + count]
    sigs = refs[12 + count : 12 + count + len(counts)]
    outs = refs[12 + count + len(counts) : 12 + count + len(counts) + inner]
    val_t2, val_t_lo, st_sq, st_t_sq, adj, adj_n, result = refs[12 + count + len(counts) + inner :]
    heads, rows, dh = num_ref.shape
    feat_dim = sig_ref.shape[2]
    ratio = heads // groups
    total = outer * inner
    q_rows, k_rows = ratio * dh // total, dh // total
    outer_me, inner_me = flags[count], flags[count + 1]
    columns = slice(group * dh, (group + 1) * dh)
    val_columns = slice((groups + group) * dh, (groups + group + 1) * dh)

    def place(s):
        i, j = lax.div(s, inner), lax.rem(s, inner)
        return lax.rem(j - inner_me + inner, inner), lax.rem(i - outer_me + outer, outer)

    hi, lo = split(kv_ref[:, val_columns].T)
    val_t2[...] = tall(hi)
    val_t_lo[...] = lo
    st_sq[...] = square(st_ref[group])
    st_t_sq[...] = square(st_ref[group].T)
    adj[...] = jnp.zeros_like(adj)
    adj_n[...] = jnp.zeros_like(adj_n)
    norm_prev = jnp.sum(nm_ref[group], axis=0, keepdims=True)
    causal = causal_mask(rows)

    def some_heads(j, _):
        each = [group * ratio + j * pair + p for p in range(pair)]
        teacher = [(acc_ref[h] / stat_ref[h, 1:2, :]).T for h in each]
        qfw = [qf_ref[h] for h in each]
        qf = [x[:, :feat_dim].astype(F32) + x[:, feat_dim:].astype(F32) for x in qfw]
        num = [num_ref[h] + fold(mm(x, st_sq[...])) for x, h in zip(qfw, each)]
        inv = [1.0 / row_sum(part_ref[h] + x * norm_prev) for x, h in zip(qf, each)]
        student = [x * y for x, y in zip(num, inv)]
        mismatch = [x - y for x, y in zip(student, teacher)]
        gn = [wide(x * y) for x, y in zip(mismatch, inv)]
        gd = [-row_sum(x * y) * z for x, y, z in zip(mismatch, student, inv)]
        coupling = [mm(x, val_t2[...]) + mm(x[:, :dh], val_t_lo[...]) for x in gn]
        coupling = [split(jnp.where(causal, x + y, 0.0)) for x, y in zip(coupling, gd)]
        feat = feat_ref[group]
        gqf = [
            fold(mm(hi, feat)) + mm(lo, feat[:, :feat_dim]) + fold(mm(x, st_t_sq[...])) + y * norm_prev
            for (hi, lo), x, y in zip(coupling, gn, gd)
        ]
        for (hi, lo), x, y in zip(coupling, gn, qfw):
            left_hi = jnp.concatenate([hi, x[:, :dh]], axis=1)
            left_lo = jnp.concatenate([lo, x[:, dh:]], axis=1)
            adj[...] += fold(mm(left_hi, y, TN)) + mm(left_lo, y[:, :feat_dim], TN)
        for x, y in zip(qf, gd):
            adj_n[...] += jnp.sum((x * y).reshape(-1, 8, feat_dim), axis=0)
        back = [wide(x * sig_ref[h]) for x, h in zip(gqf, each)]
        for p, (x, h) in enumerate(zip(back, each)):
            hi, lo = split(q_ref[:, pl.ds(pl.multiple_of(h * dh, dh), dh)])
            grad = fold(mm(hi, x, TN)) + mm(lo, x[:, :feat_dim], TN)
            first = (j * pair + p) * (dh // q_rows)
            for k in range(dh // q_rows):
                e, f = place(first + k)
                result[e, f, :q_rows, :] = grad[k * q_rows : (k + 1) * q_rows]
        return 0

    lax.fori_loop(0, ratio // pair, some_heads, 0)

    def key_side(keys, x):
        xw = wide(x)
        hi, lo = split(keys)
        return fold(mm(hi, xw, TN)) + mm(lo, xw[:, :feat_dim], TN)

    adj_sq = square(adj[rows:])
    adj_norm = jnp.sum(adj_n[...], axis=0, keepdims=True)
    grad_k = key_side(kv_ref[:, columns], adj[:rows] * sig_k_ref[group])
    b = 0
    for stage, number in enumerate(counts):
        for k in range(number):
            grad = fold(mm(wide(blocks[b][:, val_columns]), adj_sq)) + adj_norm
            more = key_side(blocks[b][:, columns], grad * sigs[stage][k, group])
            grad_k = grad_k + jnp.where(flags[b] > 0, more, 0.0)
            b += 1
    for s in range(total):
        e, f = place(s)
        result[e, f, q_rows:, :] = grad_k[s * k_rows : (s + 1) * k_rows]
    for e in range(inner):
        outs[e][...] = result[e]


def learn(group, flags, q, own, state, mine, blocks, sigs, sizes, pair):
    groups, heads, outer, inner, dh, feat = sizes
    rows = own.shape[0]
    total = outer * inner
    share = (heads // groups + 1) * dh // total
    counts = tuple(x.shape[0] for x in sigs)
    stat, acc, st, nm = state
    args = [flags, q, own, st, nm, stat, acc, *mine, *blocks, *sigs]
    return vmem_call(
        functools.partial(learn_kernel, group, groups, counts, pair, outer, inner),
        args,
        [jax.ShapeDtypeStruct((outer, share, feat), F32)] * inner,
        [
            pltpu.VMEM((2 * dh, rows), BF16),
            pltpu.VMEM((dh, rows), BF16),
            pltpu.VMEM((2 * feat, 2 * dh), BF16),
            pltpu.VMEM((2 * dh, 2 * feat), BF16),
            pltpu.VMEM((rows + dh, feat), F32),
            pltpu.VMEM((8, feat), F32),
            pltpu.VMEM((inner, outer, share, feat), F32),
        ],
        heads // groups * 40 * rows * rows * dh,
    )


def pack_kernel(k_ref, v_ref, out_ref):
    width = k_ref.shape[1]
    out_ref[:, :width] = k_ref[...]
    out_ref[:, width:] = v_ref[...]


def piece_kernel(*refs):
    out = refs[-1]
    rows = refs[0].shape[0]
    value = functools.reduce(jnp.add, [r[...] for r in refs[:-1]])
    out[:rows, :] = value
    squares = jnp.sum((value * value).reshape(-1, 8, value.shape[1]), axis=0)
    out[rows:, :] = squares


def finish_kernel(groups, inner, outer, q_rows, k_rows, count, where, *refs):
    squares = refs[0]
    lines = refs[1 : 1 + groups * inner]
    gq_ref, gk_ref = refs[1 + groups * inner :]
    mean = jnp.sum(jnp.sum(squares[...], axis=0, keepdims=True), axis=1, keepdims=True) / count
    factor = 1.0 / jnp.sqrt(mean + EPSILON)
    total = outer * inner
    for g in range(groups):
        for e in range(inner):
            for f in range(outer):
                i = lax.rem(where[0] - f + outer, outer)
                j = lax.rem(where[1] - e + inner, inner)
                s = i * inner + j
                line = lines[g * inner + e]
                q_at = pl.multiple_of((g * total + s) * q_rows, q_rows)
                k_at = pl.multiple_of((g * total + s) * k_rows, k_rows)
                gq_ref[pl.ds(q_at, q_rows), :] = line[f, :q_rows, :] * factor
                gk_ref[pl.ds(k_at, k_rows), :] = line[f, q_rows : q_rows + k_rows, :] * factor


def butterfly(value, axis):
    size = lax.axis_size(axis)
    hop = 1
    while hop < size:
        value = value + ppermute(value, [(s, s ^ hop) for s in range(size)], axis)
        hop *= 2
    return value


def ppermute(value, pairs, axis="seq"):
    return lax.ppermute(value, axis, pairs)


def on_device(queries, key_heads, value_heads, query_map, key_map):
    heads = query_map.shape[0]
    groups, dh, feat = key_map.shape
    rows = queries.shape[0]
    ratio = heads // groups
    pair = 2 if ratio % 2 == 0 else 1
    total = lax.axis_size("seq")
    inner = 1 << ((total.bit_length() - 1) // 2)
    outer = total // inner
    me = lax.axis_index("seq")
    outer_me, inner_me = me // inner, me % inner
    at = lambda i, j: i * inner + j
    own = pl.pallas_call(
        pack_kernel,
        out_shape=jax.ShapeDtypeStruct((rows, 2 * groups * dh), F32),
        out_specs=pl.BlockSpec(memory_space=pltpu.VMEM),
        compiler_params=pltpu.CompilerParams(vmem_limit_bytes=LIMIT),
        name="pack",
    )(key_heads, value_heads)

    along, across = [], []
    moving = own
    for i in range(outer):
        if i > 0:
            pairs = [(at(p, j), at(p + 1, j)) for p in range(outer - 1) for j in range(inner)]
            moving = ppermute(moving, pairs)
        along.append((moving, outer_me >= i))
        side = []
        last = i == outer - 1 and i > 0
        for d in range(1, inner):
            pairs = [
                (at(p, (j + d) % inner), at(p, j))
                for p in range(outer)
                for j in range(inner)
            ]
            flag = outer_me >= i if i > 0 else (inner_me + d) % inner < inner_me
            if last and rows % 16 == 0:
                half = rows // 2
                ahead = across[i - 1][d - 1][0]
                line = [(at(p, j), at(p + 1, j)) for p in range(outer - 1) for j in range(inner)]
                parts = [ppermute(moving[:half], pairs), ppermute(ahead[half:], line)]
                side.append((jnp.concatenate(parts, axis=0), flag))
            else:
                side.append((ppermute(moving, pairs), flag))
        across.append(side)

    always = jnp.ones((1,), jnp.int32)
    turned, stat, acc = attend(queries, [own], always, key_map, None, heads, 4)
    state = [stat, acc, jnp.zeros((groups, feat, dh), F32), jnp.zeros((groups, 8, feat), F32)]
    mine = local(queries, own, query_map, key_map, pair)
    blocks, flags, sigs = [], [], []
    for i in range(1, outer + 1):
        now = (along[i : i + 1] if i < outer else []) + across[i - 1]
        if now:
            here = [b for b, _ in now]
            on = jnp.stack([f.astype(jnp.int32) for _, f in now])
            *state, sig = attend(turned, here, on, key_map, state, heads, 4)
            sigs.append(sig)
            blocks += here
            flags.append(on)
    flags = jnp.concatenate(flags)

    total_heads = heads * lax.axis_size("head")
    cells = (total_heads + groups * lax.axis_size("head")) * dh * feat
    places = jnp.stack([outer_me, inner_me]).astype(jnp.int32)
    scalars = jnp.concatenate([flags, places])
    share = (ratio + 1) * dh // total
    sizes = (groups, heads, outer, inner, dh, feat)
    over = lambda d: [(at(p, j), at(p, (j + d) % inner)) for p in range(outer) for j in range(inner)]
    up = lambda d: [(at(p, j), at((p + d) % outer, j)) for p in range(outer) for j in range(inner)]
    vmem = pl.BlockSpec(memory_space=pltpu.VMEM)
    lines = []
    for g in range(groups):
        parts = learn(g, scalars, queries, own, state, mine, blocks, sigs, sizes, pair)
        taken = [ppermute(parts[d], over(d)) for d in range(1, inner)]
        half = [functools.reduce(jnp.add, [x[f] for x in taken], parts[0][f]) for f in range(outer)]
        taken = [ppermute(half[d], up(d)) for d in range(1, outer)]
        piece = pl.pallas_call(
            piece_kernel,
            out_shape=jax.ShapeDtypeStruct((share + 8, feat), F32),
            in_specs=[vmem] * outer,
            out_specs=vmem,
            compiler_params=pltpu.CompilerParams(vmem_limit_bytes=LIMIT),
        )(half[0], *taken)
        found = [piece] + [ppermute(piece, up(d)) for d in range(1, outer)]
        lines.append(jnp.stack(found))

    squares = sum(x[f, share:] for x in lines for f in range(outer))
    squares = butterfly(squares, "head")
    squares = functools.reduce(jnp.add, [ppermute(squares, over(d)) for d in range(1, inner)], squares)
    crossed = [[line] + [ppermute(line, over(d)) for d in range(1, inner)] for line in lines]
    crossed = [x for group in crossed for x in group]
    q_rows, k_rows = ratio * dh // total, dh // total
    gq, gk = pl.pallas_call(
        functools.partial(finish_kernel, groups, inner, outer, q_rows, k_rows, cells),
        out_shape=[
            jax.ShapeDtypeStruct((heads * dh, feat), F32),
            jax.ShapeDtypeStruct((groups * dh, feat), F32),
        ],
        in_specs=[pl.BlockSpec(memory_space=pltpu.SMEM)] + [vmem] * (1 + len(crossed)),
        compiler_params=pltpu.CompilerParams(vmem_limit_bytes=LIMIT),
        name="finish",
    )(places, squares, *crossed)
    return gq.reshape(heads, dh, feat), gk.reshape(groups, dh, feat)


def solution(mesh):
    placed = (
        P("seq", "head"),
        P("seq", "head"),
        P("seq", "head"),
        P("head", None, None),
        P("head", None, None),
    )

    return jax.shard_map(
        on_device,
        mesh=mesh,
        in_specs=placed,
        out_specs=(P("head", None, None), P("head", None, None)),
        check_vma=False,
    )
```
